256 devices in a mesh: rows: 64 (over z, x, core), cols: 4 (over y).
Axes of the slice: x: 4, y: 4, z: 8, core: 2. Of those that a mesh axis runs over, the one named last changes fastest.
Arguments:
- h_blocks: float32 [512, 48, 64, 64], P('rows', 'cols'), may hold values from -0.109375 to 0.109375
- p_blocks: float32 [512, 48, 64, 64], P('rows', 'cols'), may hold values from -0.109375 to 0.109375
- h_fetch: int32 [64, 64, 2], P('rows'), may hold values from 0 to 7
- p_fetch: int32 [64, 64, 2], P('rows'), may hold values from 0 to 7
- h_slot: int32 [512, 48], P('rows'), may hold values from 0 to 127
- p_slot: int32 [512, 48], P('rows'), may hold values from 0 to 127
- p_panel: float32 [32768, 1024], P('rows', 'cols'), may hold values from -6 to 6
Outputs:
- w_panel: float32 [32768, 1024], P('rows', 'cols')
The draws below stay inside these ranges and needn't reach their ends.
Inputs may be any that keep to these rules, and one draw needn't show every extreme that they name: `p_fetch`: local block rows of the owner. `h_slot`: slot 2 * o + c names entry c of the owner o's fetch list. `p_slot`: slot 2 * o + c names entry c of the owner o's fetch list.
All inputs are finite; a program needn't handle non-finite values.
Results may differ from the reference program's by a relative error of at most 0.000098.
Values sent between devices are 32-bit elements; how exact they have to be, the bound alone decides.
No kernel may reach another device: no remote copies, remote signals or barrier semaphores. Data moves between devices by JAX's collectives and lax.ppermute only.
A program may use at most 128 MiB of HBM per device.

```python
import jax
import jax.numpy as jnp
from jax import lax

B = 64
NB_DEV = 8
KB = 48
CAP = 2
NBR = 512
SLOTS = 128
PC = 16
N_ROWS = 64


def set_ends(array, own_key, low, top_value):
    place = [jax.random.randint(jax.random.fold_in(own_key, axis), (), 0, length) for axis, length in enumerate(array.shape)]
    widest = array.shape.index(max(array.shape))
    neighbour = place[:widest] + [(place[widest] + 1) % array.shape[widest]] + place[widest + 1:]
    return array.at[tuple(place)].set(low).at[tuple(neighbour)].set(top_value)


def shard_levels(own_key, extent, pieces, low, largest):
    loudness, own = 1.0, jax.random.fold_in(own_key, 6)
    for dim, parts in pieces:
        heights = jnp.exp(jax.random.uniform(jax.random.fold_in(own, dim), (parts,), jnp.float32, low / len(pieces), largest / len(pieces)))
        loudness = loudness * jnp.repeat(heights, extent[dim] // parts).reshape([-1 if axis == dim else 1 for axis in range(len(extent))])
    return loudness


def noise(key, shape, scale, bound, pieces=(), kind=jnp.bfloat16):
    array = scale * jax.random.normal(key, shape, jnp.float32)
    if pieces:
        array = array * shard_levels(key, shape, pieces, -0.22, 0.18)
    return jnp.clip(array, -bound, bound).astype(kind)


def setup_inputs(seed: int = 0) -> dict:
    key_of = jax.random.split(jax.random.key(seed), 8)
    return {
        "h_blocks": noise(key_of[0], (NBR, KB, B, B), (KB * B) ** -0.5, 0.109375, ((0, 64), (1, 4)), jnp.float32),
        "p_blocks": noise(key_of[1], (NBR, KB, B, B), (KB * B) ** -0.5, 0.109375, ((0, 64), (1, 4)), jnp.float32),
        "h_fetch": set_ends(jax.random.randint(key_of[2], (N_ROWS, N_ROWS, CAP), 0, NB_DEV), jax.random.fold_in(key_of[2], 1), 0, NB_DEV - 1).astype(jnp.int32),
        "p_fetch": set_ends(jax.random.randint(key_of[3], (N_ROWS, N_ROWS, CAP), 0, NB_DEV), jax.random.fold_in(key_of[3], 1), 0, NB_DEV - 1).astype(jnp.int32),
        "h_slot": set_ends(jax.random.randint(key_of[4], (NBR, KB), 0, SLOTS), jax.random.fold_in(key_of[4], 1), 0, SLOTS - 1).astype(jnp.int32),
        "p_slot": set_ends(jax.random.randint(key_of[5], (NBR, KB), 0, SLOTS), jax.random.fold_in(key_of[5], 1), 0, SLOTS - 1).astype(jnp.int32),
        "p_panel": noise(key_of[6], (NBR * B, PC * B), 1.0, 6.0, ((0, 64), (1, 4)), jnp.float32),
    }


highest = lax.Precision.HIGHEST


def sparse_product(block_list, fetch_lists, slot_lists, right_side):
    nbr_all = block_list.shape[0]
    block_size = block_list.shape[2]
    columns = right_side.shape[1]
    n_owners = fetch_lists.shape[0]
    own_rows = nbr_all // n_owners
    cap_size = fetch_lists.shape[2]
    stacked = right_side.reshape(nbr_all, block_size, columns)
    device_ids = (jnp.arange(nbr_all, dtype=jnp.int32) // own_rows).astype(jnp.int32)
    owners = (slot_lists // cap_size).astype(jnp.int32)
    position = (slot_lists % cap_size).astype(jnp.int32)
    local_row = fetch_lists[device_ids[:, None], owners, position]
    targets = (owners * own_rows + local_row).astype(jnp.int32)

    def per_row(pair_in):
        row_blocks_in, row_targets = pair_in
        return jnp.einsum("jab,jbc->ac", row_blocks_in, stacked[row_targets], precision=highest)

    result = lax.map(per_row, (block_list, targets))
    return result.reshape(nbr_all * block_size, columns)


def reference(h_blocks, p_blocks, h_fetch, p_fetch, h_slot, p_slot, p_panel):
    middle = sparse_product(h_blocks, h_fetch, h_slot, p_panel)
    return sparse_product(p_blocks, p_fetch, p_slot, middle)
```

```python
import functools

import jax
import jax.numpy as jnp
from jax import lax
from jax.experimental import pallas as pl
from jax.experimental.pallas import tpu as pltpu
from jax.sharding import PartitionSpec as P

NZ, NX, NC, NY = 8, 4, 2, 4
B, HALF = 64, 128
GROUPS = ((0,), (7, 1), (6, 2), (5, 3, 4))


def rows_shift(array, dz=0, dx=0, dc=0):
    pairs = []
    for z in range(NZ):
        for x in range(NX):
            for c in range(NC):
                target = (((z + dz) % NZ) * NX + (x + dx) % NX) * NC + (c ^ dc)
                pairs.append(((z * NX + x) * NC + c, target))
    return lax.ppermute(array, "rows", pairs)


def cols_shift(array, dy):
    return lax.ppermute(array, "cols", [(y, (y + dy) % NY) for y in range(NY)])


def pack_kernel(offsets, meta, fetch, *refs):
    pieces = refs[: len(offsets)]
    outs = refs[len(offsets) : len(offsets) + 3]
    sems = refs[-1]
    z, x, c = meta[0], meta[1], meta[2]
    for s in range(3):
        for n, off in enumerate(offsets):
            zp = (z + off) % NZ
            for cc in range(2):
                owner = (zp * NX + x) * NC + (c ^ cc)
                for l in range(2):
                    for f in range(2):
                        row = cc * 8 + fetch[s * 2 + l, owner * 2 + f]
                        pltpu.make_async_copy(
                            pieces[n].at[row], outs[s].at[n * 8 + cc * 4 + l * 2 + f], sems.at[s]
                        ).start()
    for s in range(3):
        pltpu.make_async_copy(outs[s], outs[s], sems.at[s]).wait()


def pack(offsets, meta, fetch, pieces):
    shape = jax.ShapeDtypeStruct((len(offsets) * 8,) + pieces[0].shape[1:], jnp.float32)
    return pl.pallas_call(
        functools.partial(pack_kernel, offsets),
        out_shape=[shape] * 3,
        grid_spec=pltpu.PrefetchScalarGridSpec(
            num_scalar_prefetch=2,
            grid=(1,),
            in_specs=[pl.BlockSpec(memory_space=pl.ANY)] * len(pieces),
            out_specs=[pl.BlockSpec(memory_space=pl.ANY)] * 3,
            scratch_shapes=[pltpu.SemaphoreType.DMA((3,))],
        ),
        name="pack",
    )(meta, fetch, *pieces)


def product_kernel(meta, fetch, pos, *refs):
    own_blocks, partner_blocks = refs[:4], refs[4:8]
    line = refs[8:16]
    remote = refs[16:28]
    out, slabs, split, sems = refs[28:]
    z, x, c, y = meta[0], meta[1], meta[2], meta[3]
    step = pl.program_id(0)

    @pl.when(step == 0)
    def _():
        for s in range(1, NX):
            for g, offsets in enumerate(GROUPS):
                for n, off in enumerate(offsets):
                    pltpu.make_async_copy(
                        remote[g * 3 + s - 1].at[pl.ds(n * 8, 8)],
                        slabs.at[pl.ds(((NX - s) * NZ + off) * 8, 8)],
                        sems.at[NX - s],
                    ).start()
        for off in range(NZ):
            zp = (z + off) % NZ
            for cc in range(2):
                owner = (zp * NX + x) * NC + (c ^ cc)
                for l in range(2):
                    for f in range(2):
                        row = cc * 8 + fetch[l, owner * 2 + f]
                        pltpu.make_async_copy(
                            line[off].at[row], slabs.at[off * 8 + cc * 4 + l * 2 + f], sems.at[0]
                        ).start()
        for s in range(NX):
            part = slabs.at[pl.ds(s * 64, 64)]
            pltpu.make_async_copy(part, part, sems.at[s]).wait()

            def convert(i, carry):
                value = slabs[i]
                high = value.astype(jnp.bfloat16)
                split[i, :, :HALF] = high
                split[i, :, HALF:] = (value - high.astype(jnp.float32)).astype(jnp.bfloat16)
                return carry

            lax.fori_loop(s * 64, s * 64 + 64, convert, 0, unroll=4)

    for l, blocks in enumerate((own_blocks, partner_blocks)):
        total = jnp.zeros((2 * B, 2 * HALF), jnp.float32)
        for q, off in enumerate((0, 3, 1, 2)):
            base = (l * 8 + step) * 48 + ((y + off) % NY) * 12
            for t in range(3):
                left = blocks[q][0, :, t * 256 : (t + 1) * 256]
                high = left.astype(jnp.bfloat16)
                low = (left - high.astype(jnp.float32)).astype(jnp.bfloat16)
                right = jnp.concatenate([split[pos[base + t * 4 + j]] for j in range(4)], axis=0)
                total = total + jnp.dot(
                    jnp.concatenate([high, low], axis=0), right, preferred_element_type=jnp.float32
                )
        upper, lower = total[:B], total[B:]
        out[l, 0] = upper[:, :HALF] + (upper[:, HALF:] + (lower[:, :HALF] + lower[:, HALF:]))


def product(meta, fetch, pos, own_blocks, partner_blocks, line, remote):
    block = pl.BlockSpec((1, B, 768), lambda i, *_: (i, 0, 0))
    anywhere = pl.BlockSpec(memory_space=pl.ANY)
    return pl.pallas_call(
        product_kernel,
        out_shape=jax.ShapeDtypeStruct((2, 8, B, HALF), jnp.float32),
        grid_spec=pltpu.PrefetchScalarGridSpec(
            num_scalar_prefetch=3,
            grid=(8,),
            in_specs=[block] * 8 + [anywhere] * 20,
            out_specs=pl.BlockSpec((2, 1, B, HALF), lambda i, *_: (0, i, 0, 0)),
            scratch_shapes=[
                pltpu.VMEM((256, B, HALF), jnp.float32),
                pltpu.VMEM((256, B, 2 * HALF), jnp.bfloat16),
                pltpu.SemaphoreType.DMA((NX,)),
            ],
        ),
        compiler_params=pltpu.CompilerParams(dimension_semantics=("arbitrary",)),
        name="product",
    )(meta, fetch, pos, *own_blocks, *partner_blocks, *line, *remote)


def fetch_rows(own, meta, fetch_x):
    line = {0: own}
    up = down = own
    for n in range(1, 4):
        up, down = rows_shift(up, dz=1), rows_shift(down, dz=-1)
        line[NZ - n], line[n] = up, down
    line[4] = jnp.concatenate([rows_shift(up[:8], dz=1), rows_shift(down[8:], dz=-1)], axis=0)
    remote = []
    for offsets in GROUPS:
        packed = pack(offsets, meta, fetch_x, [line[off] for off in offsets])
        remote.extend(rows_shift(packed[s], dx=s + 1) for s in range(3))
    return [line[off] for off in range(NZ)], remote


def gather_blocks(blocks):
    mine = blocks.transpose(0, 2, 1, 3).reshape(8, B, 768)
    up, down = cols_shift(mine, 1), cols_shift(mine, -1)
    far = jnp.concatenate([cols_shift(up[:4], 1), cols_shift(down[4:], -1)], axis=0)
    own = [mine, up, down, far]
    return own, [rows_shift(piece, dc=1) for piece in own]


def positions(slots, z, x, c):
    owner, f = slots // 2, slots % 2
    zp, xp, cp = owner // 8, (owner // 2) % 4, owner % 2
    l = lax.broadcasted_iota(jnp.int32, slots.shape, 0) // 8
    return ((((xp - x) % NX) * NZ + (zp - z) % NZ) * 8 + (cp ^ c) * 4 + l * 2 + f).reshape(-1)


def body(h_blocks, p_blocks, h_fetch, p_fetch, h_slot, p_slot, p_panel):
    r = lax.axis_index("rows").astype(jnp.int32)
    z, x, c = r // 8, (r // 2) % 4, r % 2
    meta = jnp.stack([z, x, c, lax.axis_index("cols").astype(jnp.int32)])

    left, right = p_panel[:, :HALF], p_panel[:, HALF:]
    keep, give = jnp.where(c == 0, left, right), jnp.where(c == 0, right, left)
    own = jnp.concatenate([keep, rows_shift(give, dc=1)], axis=0).reshape(16, B, HALF)

    pad = ((0, 0), (0, 80))
    numbers = jnp.concatenate(
        [h_fetch.reshape(1, 128), p_fetch.reshape(1, 128), jnp.pad(h_slot, pad), jnp.pad(p_slot, pad)], axis=0
    )
    other = rows_shift(numbers, dc=1)
    lists = jnp.concatenate([numbers[:2], other[:2]], axis=0)
    along = [rows_shift(lists, dx=-s) for s in range(1, 4)]

    h_own, h_partner = gather_blocks(h_blocks)
    p_own, p_partner = gather_blocks(p_blocks)

    for n, (mine, partner) in enumerate(((h_own, h_partner), (p_own, p_partner))):
        fetch = lists[n::2]
        fetch_x = jnp.concatenate([a[n::2] for a in along], axis=0)
        low = 2 + 8 * n
        pos = positions(jnp.concatenate([numbers[low : low + 8, :48], other[low : low + 8, :48]], axis=0), z, x, c)
        line, remote = fetch_rows(own, meta, fetch_x)
        own = product(meta, fetch, pos, mine, partner, line, remote).reshape(16, B, HALF)

    result = own.reshape(2, 512, HALF)
    back = rows_shift(result[1], dc=1)
    return jnp.where(
        c == 0,
        jnp.concatenate([result[0], back], axis=1),
        jnp.concatenate([back, result[0]], axis=1),
    )


def solution(mesh):
    in_specs = (
        P("rows", "cols", None, None),
        P("rows", "cols", None, None),
        P("rows", None, None),
        P("rows", None, None),
        P("rows", None),
        P("rows", None),
        P("rows", "cols"),
    )
    return jax.shard_map(body, mesh=mesh, in_specs=in_specs, out_specs=P("rows", "cols"), check_vma=False)
```

```python
import functools

import jax
import jax.numpy as jnp
from jax import lax
from jax.experimental import pallas as pl
from jax.experimental.pallas import tpu as pltpu
from jax.sharding import PartitionSpec as P

NZ, NX, NC, NY = 8, 4, 2, 4
B, HALF = 64, 128
GROUPS = ((0,), (7, 1), (6, 2), (5, 3, 4))


def rows_shift(array, dz=0, dx=0, dc=0):
    pairs = []
    for z in range(NZ):
        for x in range(NX):
            for c in range(NC):
                target = (((z + dz) % NZ) * NX + (x + dx) % NX) * NC + (c ^ dc)
                pairs.append(((z * NX + x) * NC + c, target))
    return lax.ppermute(array, "rows", pairs)


def cols_shift(array, dy):
    return lax.ppermute(array, "cols", [(y, (y + dy) % NY) for y in range(NY)])


def pack_kernel(offsets, meta, fetch, *refs):
    pieces = refs[: len(offsets)]
    outs = refs[len(offsets) : len(offsets) + 3]
    sems = refs[-1]
    z, x, c = meta[0], meta[1], meta[2]
    for s in range(3):
        for n, off in enumerate(offsets):
            zp = (z + off) % NZ
            for cc in range(2):
                owner = (zp * NX + x) * NC + (c ^ cc)
                for l in range(2):
                    for f in range(2):
                        row = cc * 8 + fetch[s * 2 + l, owner * 2 + f]
                        pltpu.make_async_copy(
                            pieces[n].at[row], outs[s].at[n * 8 + cc * 4 + l * 2 + f], sems.at[s]
                        ).start()
    for s in range(3):
        pltpu.make_async_copy(outs[s], outs[s], sems.at[s]).wait()


def pack(offsets, meta, fetch, pieces):
    shape = jax.ShapeDtypeStruct((len(offsets) * 8,) + pieces[0].shape[1:], jnp.float32)
    return pl.pallas_call(
        functools.partial(pack_kernel, offsets),
        out_shape=[shape] * 3,
        grid_spec=pltpu.PrefetchScalarGridSpec(
            num_scalar_prefetch=2,
            grid=(1,),
            in_specs=[pl.BlockSpec(memory_space=pl.ANY)] * len(pieces),
            out_specs=[pl.BlockSpec(shape.shape, lambda *_: (0, 0, 0))] * 3,
            scratch_shapes=[pltpu.SemaphoreType.DMA((3,))],
        ),
        name="pack",
    )(meta, fetch, *pieces)


def product_kernel(meta, fetch, pos, *refs):
    own_blocks, partner_blocks = refs[:4], refs[4:8]
    line = refs[8:16]
    remote = refs[16:28]
    out, slabs, split, sems = refs[28:]
    z, x, c, y = meta[0], meta[1], meta[2], meta[3]
    step = pl.program_id(0)

    @pl.when(step == 0)
    def _():
        for s in range(1, NX):
            for g, offsets in enumerate(GROUPS):
                for n, off in enumerate(offsets):
                    pltpu.make_async_copy(
                        remote[g * 3 + s - 1].at[pl.ds(n * 8, 8)],
                        slabs.at[pl.ds(((NX - s) * NZ + off) * 8, 8)],
                        sems.at[NX - s],
                    ).start()
        for off in range(NZ):
            zp = (z + off) % NZ
            for cc in range(2):
                owner = (zp * NX + x) * NC + (c ^ cc)
                for l in range(2):
                    for f in range(2):
                        row = cc * 8 + fetch[l, owner * 2 + f]
                        pltpu.make_async_copy(
                            line[off].at[row], slabs.at[off * 8 + cc * 4 + l * 2 + f], sems.at[0]
                        ).start()
        for s in range(NX):
            part = slabs.at[pl.ds(s * 64, 64)]
            pltpu.make_async_copy(part, part, sems.at[s]).wait()

            def convert(i, carry):
                value = slabs[i]
                high = value.astype(jnp.bfloat16)
                split[i, :, :HALF] = high
                split[i, :, HALF:] = (value - high.astype(jnp.float32)).astype(jnp.bfloat16)
                return carry

            lax.fori_loop(s * 64, s * 64 + 64, convert, 0, unroll=4)

    for l, blocks in enumerate((own_blocks, partner_blocks)):
        total = jnp.zeros((2 * B, 2 * HALF), jnp.float32)
        for q, off in enumerate((0, 3, 1, 2)):
            base = (l * 8 + step) * 48 + ((y + off) % NY) * 12
            for t in range(3):
                left = blocks[q][0, :, t * 256 : (t + 1) * 256]
                high = left.astype(jnp.bfloat16)
                low = (left - high.astype(jnp.float32)).astype(jnp.bfloat16)
                right = jnp.concatenate([split[pos[base + t * 4 + j]] for j in range(4)], axis=0)
                total = total + jnp.dot(
                    jnp.concatenate([high, low], axis=0), right, preferred_element_type=jnp.float32
                )
        upper, lower = total[:B], total[B:]
        out[l, 0] = upper[:, :HALF] + (upper[:, HALF:] + (lower[:, :HALF] + lower[:, HALF:]))


def product(meta, fetch, pos, own_blocks, partner_blocks, line, remote):
    block = pl.BlockSpec((1, B, 768), lambda i, *_: (i, 0, 0))
    anywhere = pl.BlockSpec(memory_space=pl.ANY)
    return pl.pallas_call(
        product_kernel,
        out_shape=jax.ShapeDtypeStruct((2, 8, B, HALF), jnp.float32),
        grid_spec=pltpu.PrefetchScalarGridSpec(
            num_scalar_prefetch=3,
            grid=(8,),
            in_specs=[block] * 8 + [anywhere] * 20,
            out_specs=pl.BlockSpec((2, 1, B, HALF), lambda i, *_: (0, i, 0, 0)),
            scratch_shapes=[
                pltpu.VMEM((256, B, HALF), jnp.float32),
                pltpu.VMEM((256, B, 2 * HALF), jnp.bfloat16),
                pltpu.SemaphoreType.DMA((NX,)),
            ],
        ),
        compiler_params=pltpu.CompilerParams(dimension_semantics=("arbitrary",)),
        name="product",
    )(meta, fetch, pos, *own_blocks, *partner_blocks, *line, *remote)


def fetch_rows(own, meta, fetch_x):
    line = {0: own}
    up = down = own
    for n in range(1, 4):
        up = rows_shift(up, dz=1)
        down = rows_shift(down, dz=-1)
        line[NZ - n], line[n] = up, down
    line[4] = rows_shift(up, dz=1)
    remote = []
    for offsets in GROUPS:
        packed = pack(offsets, meta, fetch_x, [line[off] for off in offsets])
        for s in range(3):
            remote.append(rows_shift(packed[s], dx=s + 1))
    return [line[off] for off in range(NZ)], remote


def gather_blocks(blocks):
    mine = blocks.transpose(0, 2, 1, 3).reshape(8, B, 768)
    own = [mine]
    for dy in (1, -1, 2):
        own.append(cols_shift(mine, dy))
    partner = []
    for piece in own:
        partner.append(rows_shift(piece, dc=1))
    return own, partner


def positions(slots, z, x, c):
    owner, f = slots // 2, slots % 2
    zp, xp, cp = owner // 8, (owner // 2) % 4, owner % 2
    l = lax.broadcasted_iota(jnp.int32, slots.shape, 0) // 8
    return ((((xp - x) % NX) * NZ + (zp - z) % NZ) * 8 + (cp ^ c) * 4 + l * 2 + f).reshape(-1)


def body(h_blocks, p_blocks, h_fetch, p_fetch, h_slot, p_slot, p_panel):
    r = lax.axis_index("rows").astype(jnp.int32)
    z, x, c = r // 8, (r // 2) % 4, r % 2
    meta = jnp.stack([z, x, c, lax.axis_index("cols").astype(jnp.int32)])

    pad = ((0, 0), (0, 80))
    numbers = jnp.concatenate(
        [h_fetch.reshape(1, 128), p_fetch.reshape(1, 128), jnp.pad(h_slot, pad), jnp.pad(p_slot, pad)], axis=0
    )
    other = rows_shift(numbers, dc=1)
    lists = jnp.concatenate([numbers[:2], other[:2]], axis=0)
    along = [rows_shift(lists, dx=-s) for s in range(1, 4)]

    left, right = p_panel[:, :HALF], p_panel[:, HALF:]
    keep, give = jnp.where(c == 0, left, right), jnp.where(c == 0, right, left)
    given = rows_shift(give, dc=1)
    own = jnp.concatenate([keep, given], axis=0).reshape(16, B, HALF)

    blocks = [gather_blocks(h_blocks), gather_blocks(p_blocks)]

    for n in range(2):
        fetch = lists[n::2]
        fetch_x = jnp.concatenate([a[n::2] for a in along], axis=0)
        low = 2 + 8 * n
        pos = positions(
            jnp.concatenate([numbers[low : low + 8, :48], other[low : low + 8, :48]], axis=0), z, x, c
        )
        line, remote = fetch_rows(own, meta, fetch_x)
        own = product(meta, fetch, pos, *blocks[n], line, remote).reshape(16, B, HALF)

    result = own.reshape(2, 512, HALF)
    back = rows_shift(result[1], dc=1)
    return jnp.where(
        c == 0,
        jnp.concatenate([result[0], back], axis=1),
        jnp.concatenate([back, result[0]], axis=1),
    )


def solution(mesh):
    in_specs = (
        P("rows", "cols", None, None),
        P("rows", "cols", None, None),
        P("rows", None, None),
        P("rows", None, None),
        P("rows", None),
        P("rows", None),
        P("rows", "cols"),
    )
    return jax.shard_map(body, mesh=mesh, in_specs=in_specs, out_specs=P("rows", "cols"), check_vma=False)
```

```python
import functools

import jax
import jax.numpy as jnp
from jax import lax
from jax.experimental import pallas as pl
from jax.experimental.pallas import tpu as pltpu
from jax.sharding import PartitionSpec as P

NZ, NX, NC, NY = 8, 4, 2, 4
B, HALF = 64, 128
GROUPS = ((0,), (7, 1), (6, 2), (5, 3, 4))

WHOLE = (False, True, False, True)


def rows_shift(array, dz=0, dx=0, dc=0):
    pairs = []
    for z in range(NZ):
        for x in range(NX):
            for c in range(NC):
                target = (((z + dz) % NZ) * NX + (x + dx) % NX) * NC + (c ^ dc)
                pairs.append(((z * NX + x) * NC + c, target))
    return lax.ppermute(array, "rows", pairs)


def cols_shift(array, dy):
    return lax.ppermute(array, "cols", [(y, (y + dy) % NY) for y in range(NY)])


def x_exchange(array):
    groups = [[(z * NX + x) * NC + c for x in range(NX)] for z in range(NZ) for c in range(NC)]
    return lax.all_to_all(array, "rows", 0, 0, axis_index_groups=groups, tiled=True)


def pack_kernel(offsets, whole, meta, fetch, *refs):
    pieces, outs = refs[: len(offsets)], refs[len(offsets) :]
    z, x, c = meta[0], meta[1], meta[2]
    for n, off in enumerate(offsets):
        base = (((z + off) & 7) * NX + x) * 4
        for s in range(NX):
            for j in range(8):
                cc, l, f = j >> 2, (j >> 1) & 1, j & 1
                row = cc * 8 + fetch[s * 2 + l, base + (c ^ cc) * 2 + f]
                if whole:
                    outs[0][(x + s) & 3, n * 8 + j] = pieces[n][row]
                else:
                    outs[s][n * 8 + j] = pieces[n][row]


def pack(offsets, whole, meta, fetch, pieces):
    part = (len(offsets) * 8,) + pieces[0].shape[1:]
    shapes = [(NX,) + part] if whole else [part] * NX
    return pl.pallas_call(
        functools.partial(pack_kernel, offsets, whole),
        out_shape=[jax.ShapeDtypeStruct(shape, jnp.float32) for shape in shapes],
        grid_spec=pltpu.PrefetchScalarGridSpec(
            num_scalar_prefetch=2,
            grid=(1,),
            in_specs=[pl.BlockSpec(pieces[0].shape, lambda *_: (0, 0, 0))] * len(pieces),
            out_specs=[pl.BlockSpec(shape, lambda *_, k=len(shape): (0,) * k) for shape in shapes],
        ),
        name="pack",
    )(meta, fetch, *pieces)


def product_kernel(meta, pos, *refs):
    arrived = iter(refs[2:-4])
    out, slabs, split, sems = refs[-4:]
    x, y = meta[1], meta[3]
    step = pl.program_id(0)

    @pl.when(step == 0)
    def _():
        for g, offsets in enumerate(GROUPS):
            block = next(arrived) if WHOLE[g] else None
            for s in range(NX):
                xp = (x - s) & 3
                part = block.at[xp] if WHOLE[g] else next(arrived)
                for n, off in enumerate(offsets):
                    pltpu.make_async_copy(
                        part.at[pl.ds(n * 8, 8)], slabs.at[pl.ds((xp * NZ + off) * 8, 8)], sems.at[xp]
                    ).start()
        for xp in range(NX):
            part = slabs.at[pl.ds(xp * 64, 64)]
            pltpu.make_async_copy(part, part, sems.at[xp]).wait()

            def convert(i, carry):
                value = slabs[i]
                high = value.astype(jnp.bfloat16)
                split[i, :, :HALF] = high
                split[i, :, HALF:] = (value - high.astype(jnp.float32)).astype(jnp.bfloat16)
                return carry

            lax.fori_loop(xp * 64, xp * 64 + 64, convert, 0, unroll=4)

    for l, blocks in enumerate(refs[:2]):
        total = jnp.zeros((2 * B, 2 * HALF), jnp.float32)
        for q, off in enumerate((0, 3, 1, 2)):
            base = (l * 8 + step) * 48 + ((y + off) % NY) * 12
            left = blocks[q, 0]
            high = left.astype(jnp.bfloat16)
            low = (left - high.astype(jnp.float32)).astype(jnp.bfloat16)
            right = jnp.concatenate([split[pos[base + j]] for j in range(12)], axis=0)
            total = total + jnp.dot(
                jnp.concatenate([high, low], axis=0), right, preferred_element_type=jnp.float32
            )
        upper, lower = total[:B], total[B:]
        out[l, 0] = upper[:, :HALF] + (upper[:, HALF:] + (lower[:, :HALF] + lower[:, HALF:]))


def product(meta, pos, own_blocks, partner_blocks, arrived):
    block = pl.BlockSpec((4, 1, B, 768), lambda i, *_: (0, i, 0, 0))
    anywhere = pl.BlockSpec(memory_space=pl.ANY)
    return pl.pallas_call(
        product_kernel,
        out_shape=jax.ShapeDtypeStruct((2, 8, B, HALF), jnp.float32),
        grid_spec=pltpu.PrefetchScalarGridSpec(
            num_scalar_prefetch=2,
            grid=(8,),
            in_specs=[block] * 2 + [anywhere] * len(arrived),
            out_specs=pl.BlockSpec((2, 1, B, HALF), lambda i, *_: (0, i, 0, 0)),
            scratch_shapes=[
                pltpu.VMEM((256, B, HALF), jnp.float32),
                pltpu.VMEM((256, B, 2 * HALF), jnp.bfloat16),
                pltpu.SemaphoreType.DMA((NX,)),
            ],
        ),
        name="product",
    )(meta, pos, own_blocks, partner_blocks, *arrived)


def fetch_rows(own, meta, fetch_x):
    line = {0: own}
    up = down = own
    for n in range(1, 4):
        up = rows_shift(up, dz=1)
        down = rows_shift(down, dz=-1)
        line[NZ - n], line[n] = up, down
    line[4] = rows_shift(up, dz=1)
    arrived = []
    for g, offsets in enumerate(GROUPS):
        packed = pack(offsets, WHOLE[g], meta, fetch_x, [line[off] for off in offsets])
        if WHOLE[g]:
            arrived.append(x_exchange(packed[0]))
            continue
        arrived.append(packed[0])
        for s in range(1, NX):
            arrived.append(rows_shift(packed[s], dx=s))
    return arrived


def turn_kernel(blocks, out):
    for t in range(6):
        out[0, :, t * 128 : (t + 1) * 128] = jnp.concatenate([blocks[0, 2 * t], blocks[0, 2 * t + 1]], axis=1)


def gather_blocks(blocks, halves):
    mine = pl.pallas_call(
        turn_kernel,
        out_shape=jax.ShapeDtypeStruct((8, B, 768), jnp.float32),
        grid=(8,),
        in_specs=[pl.BlockSpec((1, 12, B, B), lambda i: (i, 0, 0, 0))],
        out_specs=pl.BlockSpec((1, B, 768), lambda i: (i, 0, 0)),
        name="turn",
    )(blocks)
    own = [mine]
    for dy in (1, -1, 2)[: 2 if halves else 3]:
        own.append(cols_shift(mine, dy))
    if halves:
        far = []
        for n, dy in enumerate((1, -1)):
            far.append(cols_shift(own[n + 1][n * 4 : n * 4 + 4], dy))
        own.append(jnp.concatenate(far, axis=0))
    return own


def with_partner(own):
    own = jnp.stack(own)
    return own, rows_shift(own, dc=1)


def positions(slots, z, c):
    owner, f = slots // 2, slots % 2
    zp, xp, cp = owner // 8, (owner // 2) % 4, owner % 2
    l = lax.broadcasted_iota(jnp.int32, slots.shape, 0) // 8
    return ((xp * NZ + (zp - z) % NZ) * 8 + (cp ^ c) * 4 + l * 2 + f).reshape(-1)


def body(h_blocks, p_blocks, h_fetch, p_fetch, h_slot, p_slot, p_panel):
    r = lax.axis_index("rows").astype(jnp.int32)
    z, x, c = r // 8, (r // 2) % 4, r % 2
    meta = jnp.stack([z, x, c, lax.axis_index("cols").astype(jnp.int32)])

    pad = ((0, 0), (0, 80))
    numbers = jnp.concatenate(
        [h_fetch.reshape(1, 128), p_fetch.reshape(1, 128), jnp.pad(h_slot, pad), jnp.pad(p_slot, pad)], axis=0
    )
    other = rows_shift(numbers, dc=1)
    lists = jnp.concatenate([numbers[:2], other[:2]], axis=0)
    along = [lists] + [rows_shift(lists, dx=-s) for s in range(1, 4)]

    left, right = p_panel[:, :HALF], p_panel[:, HALF:]
    keep, give = jnp.where(c == 0, left, right), jnp.where(c == 0, right, left)
    given = rows_shift(give, dc=1)
    own = jnp.concatenate([keep, given], axis=0).reshape(16, B, HALF)

    blocks = [gather_blocks(h_blocks, True), gather_blocks(p_blocks, False)]

    for n in range(2):
        fetch_x = jnp.concatenate([a[n::2] for a in along], axis=0)
        low = 2 + 8 * n
        pos = positions(jnp.concatenate([numbers[low : low + 8, :48], other[low : low + 8, :48]], axis=0), z, c)
        arrived = fetch_rows(own, meta, fetch_x)
        own = product(meta, pos, *with_partner(blocks[n]), arrived).reshape(16, B, HALF)

    result = own.reshape(2, 512, HALF)
    back = rows_shift(result[1], dc=1)
    return jnp.where(
        c == 0,
        jnp.concatenate([result[0], back], axis=1),
        jnp.concatenate([back, result[0]], axis=1),
    )


def solution(mesh):
    in_specs = (
        P("rows", "cols", None, None),
        P("rows", "cols", None, None),
        P("rows", None, None),
        P("rows", None, None),
        P("rows", None),
        P("rows", None),
        P("rows", "cols"),
    )
    return jax.shard_map(body, mesh=mesh, in_specs=in_specs, out_specs=P("rows", "cols"), check_vma=False)
```

```python
import functools

import jax
import jax.numpy as jnp
from jax import lax
from jax.experimental import pallas as pl
from jax.experimental.pallas import tpu as pltpu
from jax.sharding import PartitionSpec as P

NZ, NX, NC, NY = 8, 4, 2, 4
B, HALF = 64, 128
GROUPS = ((0,), (7, 1), (6, 2), (5, 3, 4))

STARTS = (0, 1, 3, 5)
WHOLE = (False, True, False, True)


def rows_shift(array, dz=0, dx=0, dc=0):
    pairs = []
    for z in range(NZ):
        for x in range(NX):
            for c in range(NC):
                target = (((z + dz) % NZ) * NX + (x + dx) % NX) * NC + (c ^ dc)
                pairs.append(((z * NX + x) * NC + c, target))
    return lax.ppermute(array, "rows", pairs)


def cols_shift(array, dy):
    return lax.ppermute(array, "cols", [(y, (y + dy) % NY) for y in range(NY)])


def x_exchange(array):
    groups = [[(z * NX + x) * NC + c for x in range(NX)] for z in range(NZ) for c in range(NC)]
    return lax.all_to_all(array, "rows", 0, 0, axis_index_groups=groups, tiled=True)


def pack_kernel(offsets, whole, meta, fetch, *refs):
    pieces, outs = refs[: len(offsets)], refs[len(offsets) :]
    z, x, c = meta[0], meta[1], meta[2]
    for n, off in enumerate(offsets):
        base = (((z + off) & 7) * NX + x) * 4
        for s in range(NX):
            for j in range(8):
                cc, l, f = j >> 2, (j >> 1) & 1, j & 1
                row = cc * 8 + fetch[s * 2 + l, base + (c ^ cc) * 2 + f]
                if whole:
                    outs[0][(x + s) & 3, n * 8 + j] = pieces[n][row]
                else:
                    outs[s][n * 8 + j] = pieces[n][row]


def pack(offsets, whole, meta, fetch, pieces):
    part = (len(offsets) * 8,) + pieces[0].shape[1:]
    shapes = [(NX,) + part] if whole else [part] * NX
    return pl.pallas_call(
        functools.partial(pack_kernel, offsets, whole),
        out_shape=[jax.ShapeDtypeStruct(shape, jnp.float32) for shape in shapes],
        grid_spec=pltpu.PrefetchScalarGridSpec(
            num_scalar_prefetch=2,
            grid=(1,),
            in_specs=[pl.BlockSpec(pieces[0].shape, lambda *_: (0, 0, 0))] * len(pieces),
            out_specs=[pl.BlockSpec(shape, lambda *_, k=len(shape): (0,) * k) for shape in shapes],
        ),
        name="pack",
    )(meta, fetch, *pieces)


def product_kernel(meta, pos, *refs):
    arrived = iter(refs[2:-4])
    out, slabs, split, sems = refs[-4:]
    x, y = meta[1], meta[3]
    step = pl.program_id(0)

    @pl.when(step == 0)
    def _():
        for g, offsets in enumerate(GROUPS):
            block = next(arrived) if WHOLE[g] else None
            for s in range(NX):
                xp = (x - s) & 3
                part = block.at[xp] if WHOLE[g] else next(arrived)
                n = len(offsets) * 8
                pltpu.make_async_copy(part, slabs.at[pl.ds(xp * 64 + STARTS[g] * 8, n)], sems.at[xp]).start()
        for xp in range(NX):
            part = slabs.at[pl.ds(xp * 64, 64)]
            pltpu.make_async_copy(part, part, sems.at[xp]).wait()

            def convert(i, carry):
                value = slabs[i]
                high = value.astype(jnp.bfloat16)
                split[i, :, :HALF] = high
                split[i, :, HALF:] = (value - high.astype(jnp.float32)).astype(jnp.bfloat16)
                return carry

            lax.fori_loop(xp * 64, xp * 64 + 64, convert, 0, unroll=4)

    for l, blocks in enumerate(refs[:2]):
        total = jnp.zeros((2 * B, 2 * HALF), jnp.float32)
        for q, off in enumerate((0, 3, 1, 2)):
            base = (l * 8 + step) * 48 + ((y + off) % NY) * 12
            left = blocks[q, 0]
            high = left.astype(jnp.bfloat16)
            low = (left - high.astype(jnp.float32)).astype(jnp.bfloat16)
            right = jnp.concatenate([split[pos[base + j]] for j in range(12)], axis=0)
            total = total + jnp.dot(
                jnp.concatenate([high, low], axis=0), right, preferred_element_type=jnp.float32
            )
        upper, lower = total[:B], total[B:]
        out[l, 0] = upper[:, :HALF] + (upper[:, HALF:] + (lower[:, :HALF] + lower[:, HALF:]))


def product(meta, pos, own_blocks, partner_blocks, arrived):
    block = pl.BlockSpec((4, 1, B, 768), lambda i, *_: (0, i, 0, 0))
    anywhere = pl.BlockSpec(memory_space=pl.ANY)
    return pl.pallas_call(
        product_kernel,
        out_shape=jax.ShapeDtypeStruct((2, 8, B, HALF), jnp.float32),
        grid_spec=pltpu.PrefetchScalarGridSpec(
            num_scalar_prefetch=2,
            grid=(8,),
            in_specs=[block] * 2 + [anywhere] * len(arrived),
            out_specs=pl.BlockSpec((2, 1, B, HALF), lambda i, *_: (0, i, 0, 0)),
            scratch_shapes=[
                pltpu.VMEM((256, B, HALF), jnp.float32),
                pltpu.VMEM((256, B, 2 * HALF), jnp.bfloat16),
                pltpu.SemaphoreType.DMA((NX,)),
            ],
        ),
        name="product",
    )(meta, pos, own_blocks, partner_blocks, *arrived)


def fetch_rows(own, meta, fetch_x):
    line = {0: own}
    up = down = own
    for n in range(1, 4):
        up = rows_shift(up, dz=1)
        down = rows_shift(down, dz=-1)
        line[NZ - n], line[n] = up, down
    line[4] = rows_shift(up, dz=1)
    arrived = []
    for g, offsets in enumerate(GROUPS):
        packed = pack(offsets, WHOLE[g], meta, fetch_x, [line[off] for off in offsets])
        if WHOLE[g]:
            arrived.append(x_exchange(packed[0]))
            continue
        arrived.append(packed[0])
        for s in range(1, NX):
            arrived.append(rows_shift(packed[s], dx=s))
    return arrived


def turn_kernel(blocks, out):
    for t in range(6):
        out[0, :, t * 128 : (t + 1) * 128] = jnp.concatenate([blocks[0, 2 * t], blocks[0, 2 * t + 1]], axis=1)


def gather_blocks(blocks, halves):
    mine = pl.pallas_call(
        turn_kernel,
        out_shape=jax.ShapeDtypeStruct((8, B, 768), jnp.float32),
        grid=(8,),
        in_specs=[pl.BlockSpec((1, 12, B, B), lambda i: (i, 0, 0, 0))],
        out_specs=pl.BlockSpec((1, B, 768), lambda i: (i, 0, 0)),
        name="turn",
    )(blocks)
    own = [mine]
    for dy in (1, -1, 2)[: 2 if halves else 3]:
        own.append(cols_shift(mine, dy))
    if halves:
        far = []
        for n, dy in enumerate((1, -1)):
            far.append(cols_shift(own[n + 1][n * 4 : n * 4 + 4], dy))
        own.append(jnp.concatenate(far, axis=0))
    return own


def with_partner(own):
    own = jnp.stack(own)
    return own, rows_shift(own, dc=1)


def positions(slots, z, c):
    owner, f = slots // 2, slots % 2
    zp, xp, cp = owner // 8, (owner // 2) % 4, owner % 2
    l = lax.broadcasted_iota(jnp.int32, slots.shape, 0) // 8
    off = (zp - z) % NZ
    order = jnp.where(off < 4, 2 * off, jnp.where(off == 4, 7, 15 - 2 * off))
    return ((xp * NZ + order) * 8 + (cp ^ c) * 4 + l * 2 + f).reshape(-1)


def body(h_blocks, p_blocks, h_fetch, p_fetch, h_slot, p_slot, p_panel):
    r = lax.axis_index("rows").astype(jnp.int32)
    z, x, c = r // 8, (r // 2) % 4, r % 2
    meta = jnp.stack([z, x, c, lax.axis_index("cols").astype(jnp.int32)])

    pad = ((0, 0), (0, 80))
    numbers = jnp.concatenate(
        [h_fetch.reshape(1, 128), p_fetch.reshape(1, 128), jnp.pad(h_slot, pad), jnp.pad(p_slot, pad)], axis=0
    )
    other = rows_shift(numbers, dc=1)
    lists = jnp.concatenate([numbers[:2], other[:2]], axis=0)
    along = [lists] + [rows_shift(lists, dx=-s) for s in range(1, 4)]

    left, right = p_panel[:, :HALF], p_panel[:, HALF:]
    keep, give = jnp.where(c == 0, left, right), jnp.where(c == 0, right, left)
    given = rows_shift(give, dc=1)
    own = jnp.concatenate([keep, given], axis=0).reshape(16, B, HALF)

    blocks = [gather_blocks(h_blocks, True), gather_blocks(p_blocks, False)]

    for n in range(2):
        fetch_x = jnp.concatenate([a[n::2] for a in along], axis=0)
        low = 2 + 8 * n
        pos = positions(jnp.concatenate([numbers[low : low + 8, :48], other[low : low + 8, :48]], axis=0), z, c)
        arrived = fetch_rows(own, meta, fetch_x)
        own = product(meta, pos, *with_partner(blocks[n]), arrived).reshape(16, B, HALF)

    result = own.reshape(2, 512, HALF)
    back = rows_shift(result[1], dc=1)
    return jnp.where(
        c == 0,
        jnp.concatenate([result[0], back], axis=1),
        jnp.concatenate([back, result[0]], axis=1),
    )


def solution(mesh):
    in_specs = (
        P("rows", "cols", None, None),
        P("rows", "cols", None, None),
        P("rows", None, None),
        P("rows", None, None),
        P("rows", None),
        P("rows", None),
        P("rows", "cols"),
    )
    return jax.shard_map(body, mesh=mesh, in_specs=in_specs, out_specs=P("rows", "cols"), check_vma=False)
```

```python
import functools

import jax
import jax.numpy as jnp
from jax import lax
from jax.experimental import pallas as pl
from jax.experimental.pallas import tpu as pltpu
from jax.sharding import PartitionSpec as P

NZ, NX, NC, NY = 8, 4, 2, 4
B, HALF = 64, 128
GROUPS = ((0,), (7, 1), (6, 2), (5, 3, 4))

STARTS = (0, 1, 3, 5)
EARLY, LATE = 40, 24
WHOLE = (False, True, False, True)


def rows_shift(array, dz=0, dx=0, dc=0):
    pairs = []
    for z in range(NZ):
        for x in range(NX):
            for c in range(NC):
                target = (((z + dz) % NZ) * NX + (x + dx) % NX) * NC + (c ^ dc)
                pairs.append(((z * NX + x) * NC + c, target))
    return lax.ppermute(array, "rows", pairs)


def cols_shift(array, dy):
    return lax.ppermute(array, "cols", [(y, (y + dy) % NY) for y in range(NY)])


def x_exchange(array):
    groups = [[(z * NX + x) * NC + c for x in range(NX)] for z in range(NZ) for c in range(NC)]
    return lax.all_to_all(array, "rows", 0, 0, axis_index_groups=groups, tiled=True)


def pack_kernel(offsets, whole, meta, fetch, *refs):
    pieces, outs = refs[: len(offsets)], refs[len(offsets) :]
    z, x, c = meta[0], meta[1], meta[2]
    for n, off in enumerate(offsets):
        base = (((z + off) & 7) * NX + x) * 4
        for s in range(NX):
            for j in range(8):
                cc, l, f = j >> 2, (j >> 1) & 1, j & 1
                row = cc * 8 + fetch[s * 2 + l, base + (c ^ cc) * 2 + f]
                if whole:
                    outs[0][(x + s) & 3, n * 8 + j] = pieces[n][row]
                else:
                    outs[s][n * 8 + j] = pieces[n][row]


def pack(offsets, whole, meta, fetch, pieces):
    part = (len(offsets) * 8,) + pieces[0].shape[1:]
    shapes = [(NX,) + part] if whole else [part] * NX
    return pl.pallas_call(
        functools.partial(pack_kernel, offsets, whole),
        out_shape=[jax.ShapeDtypeStruct(shape, jnp.float32) for shape in shapes],
        grid_spec=pltpu.PrefetchScalarGridSpec(
            num_scalar_prefetch=2,
            grid=(1,),
            in_specs=[pl.BlockSpec(pieces[0].shape, lambda *_: (0, 0, 0))] * len(pieces),
            out_specs=[pl.BlockSpec(shape, lambda *_, k=len(shape): (0,) * k) for shape in shapes],
        ),
        name="pack",
    )(meta, fetch, *pieces)


def split_in_two(value, ref, *at):
    high = value.astype(jnp.bfloat16)
    ref[*at, :, :HALF] = high
    ref[*at, :, HALF:] = (value - high.astype(jnp.float32)).astype(jnp.bfloat16)


def early_kernel(meta, *refs):
    arrived = iter(refs[:-3])
    out, slabs, sems = refs[-3:]
    x = meta[1]
    step = pl.program_id(0)

    @pl.when(step == 0)
    def _():
        for g, offsets in enumerate(GROUPS[:-1]):
            block = next(arrived) if WHOLE[g] else None
            for s in range(NX):
                xp = (x - s) & 3
                part = block.at[xp] if WHOLE[g] else next(arrived)
                n = len(offsets) * 8
                pltpu.make_async_copy(part, slabs.at[pl.ds(xp * EARLY + STARTS[g] * 8, n)], sems.at[xp]).start()

    part = slabs.at[pl.ds(step * EARLY, EARLY)]
    pltpu.make_async_copy(part, part, sems.at[step]).wait()

    def convert(i, carry):
        split_in_two(slabs[step * EARLY + i], out, 0, i)
        return carry

    lax.fori_loop(0, EARLY, convert, 0, unroll=4)


def early_product(meta, arrived):
    return pl.pallas_call(
        early_kernel,
        out_shape=jax.ShapeDtypeStruct((NX, EARLY, B, 2 * HALF), jnp.bfloat16),
        grid_spec=pltpu.PrefetchScalarGridSpec(
            num_scalar_prefetch=1,
            grid=(NX,),
            in_specs=[pl.BlockSpec(memory_space=pl.ANY)] * len(arrived),
            out_specs=pl.BlockSpec((1, EARLY, B, 2 * HALF), lambda i, *_: (i, 0, 0, 0)),
            scratch_shapes=[
                pltpu.VMEM((NX * EARLY, B, HALF), jnp.float32),
                pltpu.SemaphoreType.DMA((NX,)),
            ],
        ),
        name="early",
    )(meta, *arrived)


def product_kernel(meta, pos, *refs):
    early, arrived, out, slabs, split, early_sems, sems = refs[2:]
    y = meta[3]
    step = pl.program_id(0)

    @pl.when(step == 0)
    def _():
        for xp in range(NX):
            pltpu.make_async_copy(arrived.at[xp], slabs.at[pl.ds(xp * LATE, LATE)], sems.at[xp]).start()
        for xp in range(NX):
            pltpu.make_async_copy(early.at[xp], split.at[pl.ds(xp * 64, EARLY)], early_sems.at[xp]).start()
        for xp in range(NX):
            part = slabs.at[pl.ds(xp * LATE, LATE)]
            pltpu.make_async_copy(part, part, sems.at[xp]).wait()

            def convert(i, carry, xp=xp):
                split_in_two(slabs[xp * LATE + i], split, xp * 64 + EARLY + i)
                return carry

            lax.fori_loop(0, LATE, convert, 0, unroll=4)
        for xp in range(NX):
            part = split.at[pl.ds(xp * 64, EARLY)]
            pltpu.make_async_copy(part, part, early_sems.at[xp]).wait()

    for l, blocks in enumerate(refs[:2]):
        total = jnp.zeros((2 * B, 2 * HALF), jnp.float32)
        for q, off in enumerate((0, 3, 1, 2)):
            base = (l * 8 + step) * 48 + ((y + off) % NY) * 12
            left = blocks[q, 0]
            high = left.astype(jnp.bfloat16)
            low = (left - high.astype(jnp.float32)).astype(jnp.bfloat16)
            right = jnp.concatenate([split[pos[base + j]] for j in range(12)], axis=0)
            total = total + jnp.dot(
                jnp.concatenate([high, low], axis=0), right, preferred_element_type=jnp.float32
            )
        upper, lower = total[:B], total[B:]
        out[l, 0] = upper[:, :HALF] + (upper[:, HALF:] + (lower[:, :HALF] + lower[:, HALF:]))


def product(meta, pos, own_blocks, partner_blocks, early, arrived):
    block = pl.BlockSpec((4, 1, B, 768), lambda i, *_: (0, i, 0, 0))
    anywhere = pl.BlockSpec(memory_space=pl.ANY)
    return pl.pallas_call(
        product_kernel,
        out_shape=jax.ShapeDtypeStruct((2, 8, B, HALF), jnp.float32),
        grid_spec=pltpu.PrefetchScalarGridSpec(
            num_scalar_prefetch=2,
            grid=(8,),
            in_specs=[block] * 2 + [anywhere] * 2,
            out_specs=pl.BlockSpec((2, 1, B, HALF), lambda i, *_: (0, i, 0, 0)),
            scratch_shapes=[
                pltpu.VMEM((NX * LATE, B, HALF), jnp.float32),
                pltpu.VMEM((256, B, 2 * HALF), jnp.bfloat16),
                pltpu.SemaphoreType.DMA((NX,)),
                pltpu.SemaphoreType.DMA((NX,)),
            ],
        ),
        name="product",
    )(meta, pos, own_blocks, partner_blocks, early, arrived)


def fetch_rows(own, meta, fetch_x):
    line = {0: own}
    up = down = own
    for n in range(1, 4):
        up = rows_shift(up, dz=1)
        down = rows_shift(down, dz=-1)
        line[NZ - n], line[n] = up, down
    line[4] = rows_shift(up, dz=1)
    arrived = []
    for g, offsets in enumerate(GROUPS):
        packed = pack(offsets, WHOLE[g], meta, fetch_x, [line[off] for off in offsets])
        if WHOLE[g]:
            arrived.append(x_exchange(packed[0]))
            continue
        arrived.append(packed[0])
        for s in range(1, NX):
            arrived.append(rows_shift(packed[s], dx=s))
    return arrived


def turn_kernel(blocks, out):
    for t in range(6):
        out[0, :, t * 128 : (t + 1) * 128] = jnp.concatenate([blocks[0, 2 * t], blocks[0, 2 * t + 1]], axis=1)


def gather_blocks(blocks, halves):
    mine = pl.pallas_call(
        turn_kernel,
        out_shape=jax.ShapeDtypeStruct((8, B, 768), jnp.float32),
        grid=(8,),
        in_specs=[pl.BlockSpec((1, 12, B, B), lambda i: (i, 0, 0, 0))],
        out_specs=pl.BlockSpec((1, B, 768), lambda i: (i, 0, 0)),
        name="turn",
    )(blocks)
    own = [mine]
    for dy in (1, -1, 2)[: 2 if halves else 3]:
        own.append(cols_shift(mine, dy))
    if halves:
        far = []
        for n, dy in enumerate((1, -1)):
            far.append(cols_shift(own[n + 1][n * 4 : n * 4 + 4], dy))
        own.append(jnp.concatenate(far, axis=0))
    return own


def with_partner(own):
    own = jnp.stack(own)
    return own, rows_shift(own, dc=1)


def positions(slots, z, c):
    owner, f = slots // 2, slots % 2
    zp, xp, cp = owner // 8, (owner // 2) % 4, owner % 2
    l = lax.broadcasted_iota(jnp.int32, slots.shape, 0) // 8
    off = (zp - z) % NZ
    order = jnp.where(off < 4, 2 * off, jnp.where(off == 4, 7, 15 - 2 * off))
    return ((xp * NZ + order) * 8 + (cp ^ c) * 4 + l * 2 + f).reshape(-1)


def body(h_blocks, p_blocks, h_fetch, p_fetch, h_slot, p_slot, p_panel):
    r = lax.axis_index("rows").astype(jnp.int32)
    z, x, c = r // 8, (r // 2) % 4, r % 2
    meta = jnp.stack([z, x, c, lax.axis_index("cols").astype(jnp.int32)])

    pad = ((0, 0), (0, 80))
    numbers = jnp.concatenate(
        [h_fetch.reshape(1, 128), p_fetch.reshape(1, 128), jnp.pad(h_slot, pad), jnp.pad(p_slot, pad)], axis=0
    )
    other = rows_shift(numbers, dc=1)
    lists = jnp.concatenate([numbers[:2], other[:2]], axis=0)
    along = [lists]
    for s in range(1, NX):
        along.append(rows_shift(lists, dx=-s))

    left, right = p_panel[:, :HALF], p_panel[:, HALF:]
    keep, give = jnp.where(c == 0, left, right), jnp.where(c == 0, right, left)
    given = rows_shift(give, dc=1)
    own = jnp.concatenate([keep, given], axis=0).reshape(16, B, HALF)

    blocks = [gather_blocks(h_blocks, True), gather_blocks(p_blocks, False)]

    for n in range(2):
        fetch_x = jnp.concatenate([a[n::2] for a in along], axis=0)
        low = 2 + 8 * n
        pos = positions(jnp.concatenate([numbers[low : low + 8, :48], other[low : low + 8, :48]], axis=0), z, c)
        arrived = fetch_rows(own, meta, fetch_x)
        early = early_product(meta, arrived[:-1])
        own = product(meta, pos, *with_partner(blocks[n]), early, arrived[-1]).reshape(16, B, HALF)

    result = own.reshape(2, 512, HALF)
    back = rows_shift(result[1], dc=1)
    return jnp.where(
        c == 0,
        jnp.concatenate([result[0], back], axis=1),
        jnp.concatenate([back, result[0]], axis=1),
    )


def solution(mesh):
    in_specs = (
        P("rows", "cols", None, None),
        P("rows", "cols", None, None),
        P("rows", None, None),
        P("rows", None, None),
        P("rows", None),
        P("rows", None),
        P("rows", "cols"),
    )
    return jax.shard_map(body, mesh=mesh, in_specs=in_specs, out_specs=P("rows", "cols"), check_vma=False)
```

```python
import functools

import jax
import jax.numpy as jnp
from jax import lax
from jax.experimental import pallas as pl
from jax.experimental.pallas import tpu as pltpu
from jax.sharding import PartitionSpec as P

NZ, NX, NC, NY = 8, 4, 2, 4
B, HALF = 64, 128
GROUPS = ((0,), (7, 1), (6, 2), (5, 3, 4))

STARTS = (0, 1, 3, 5)
EARLY, LATE = 40, 24
WHOLE = (False, True, False, True)


def rows_shift(array, dz=0, dx=0, dc=0):
    pairs = []
    for z in range(NZ):
        for x in range(NX):
            for c in range(NC):
                target = (((z + dz) % NZ) * NX + (x + dx) % NX) * NC + (c ^ dc)
                pairs.append(((z * NX + x) * NC + c, target))
    return lax.ppermute(array, "rows", pairs)


def cols_shift(array, dy):
    return lax.ppermute(array, "cols", [(y, (y + dy) % NY) for y in range(NY)])


def x_exchange(array):
    groups = [[(z * NX + x) * NC + c for x in range(NX)] for z in range(NZ) for c in range(NC)]
    return lax.all_to_all(array, "rows", 0, 0, axis_index_groups=groups, tiled=True)


def pack_kernel(offsets, whole, meta, fetch, *refs):
    pieces, outs = refs[: len(offsets)], refs[len(offsets) :]
    z, x, c = meta[0], meta[1], meta[2]
    for n, off in enumerate(offsets):
        base = (((z + off) & 7) * NX + x) * 4
        for s in range(NX):
            for j in range(8):
                cc, l, f = j >> 2, (j >> 1) & 1, j & 1
                row = cc * 8 + fetch[s * 2 + l, base + (c ^ cc) * 2 + f]
                if whole:
                    outs[0][(x + s) & 3, n * 8 + j] = pieces[n][row]
                else:
                    outs[s][n * 8 + j] = pieces[n][row]


def pack(offsets, whole, meta, fetch, pieces):
    part = (len(offsets) * 8,) + pieces[0].shape[1:]
    shapes = [(NX,) + part] if whole else [part] * NX
    return pl.pallas_call(
        functools.partial(pack_kernel, offsets, whole),
        out_shape=[jax.ShapeDtypeStruct(shape, jnp.float32) for shape in shapes],
        grid_spec=pltpu.PrefetchScalarGridSpec(
            num_scalar_prefetch=2,
            grid=(1,),
            in_specs=[pl.BlockSpec(pieces[0].shape, lambda *_: (0, 0, 0))] * len(pieces),
            out_specs=[pl.BlockSpec(shape, lambda *_, k=len(shape): (0,) * k) for shape in shapes],
        ),
        name="pack",
    )(meta, fetch, *pieces)


def split_in_two(value, ref, *at):
    high = value.astype(jnp.bfloat16)
    ref[*at, :, :HALF] = high
    ref[*at, :, HALF:] = (value - high.astype(jnp.float32)).astype(jnp.bfloat16)


def early_kernel(meta, *refs):
    arrived = iter(refs[:-3])
    out, slabs, sems = refs[-3:]
    x = meta[1]
    step = pl.program_id(0)

    @pl.when(step == 0)
    def _():
        for g, offsets in enumerate(GROUPS[:-1]):
            block = next(arrived) if WHOLE[g] else None
            for s in range(NX):
                xp = (x - s) & 3
                part = block.at[xp] if WHOLE[g] else next(arrived)
                n = len(offsets) * 8
                pltpu.make_async_copy(part, slabs.at[pl.ds(xp * EARLY + STARTS[g] * 8, n)], sems.at[xp]).start()

    part = slabs.at[pl.ds(step * EARLY, EARLY)]
    pltpu.make_async_copy(part, part, sems.at[step]).wait()

    def convert(i, carry):
        split_in_two(slabs[step * EARLY + i], out, 0, i)
        return carry

    lax.fori_loop(0, EARLY, convert, 0, unroll=4)


def early_product(meta, arrived):
    return pl.pallas_call(
        early_kernel,
        out_shape=jax.ShapeDtypeStruct((NX, EARLY, B, 2 * HALF), jnp.bfloat16),
        grid_spec=pltpu.PrefetchScalarGridSpec(
            num_scalar_prefetch=1,
            grid=(NX,),
            in_specs=[pl.BlockSpec(memory_space=pl.ANY)] * len(arrived),
            out_specs=pl.BlockSpec((1, EARLY, B, 2 * HALF), lambda i, *_: (i, 0, 0, 0)),
            scratch_shapes=[
                pltpu.VMEM((NX * EARLY, B, HALF), jnp.float32),
                pltpu.SemaphoreType.DMA((NX,)),
            ],
        ),
        name="early",
    )(meta, *arrived)


def product_kernel(ahead, meta, pos, *refs):
    if ahead:
        fetch, refs = refs[0], refs[1:]
    early, arrived, out = refs[2:5]
    slabs, split, early_sems, sems = refs[5 + NX * ahead : 9 + NX * ahead]
    y = meta[3]
    step = pl.program_id(0)

    @pl.when(step == 0)
    def _():
        for xp in range(NX):
            pltpu.make_async_copy(arrived.at[xp], slabs.at[pl.ds(xp * LATE, LATE)], sems.at[xp]).start()
        for xp in range(NX):
            pltpu.make_async_copy(early.at[xp], split.at[pl.ds(xp * 64, EARLY)], early_sems.at[xp]).start()
        for xp in range(NX):
            part = slabs.at[pl.ds(xp * LATE, LATE)]
            pltpu.make_async_copy(part, part, sems.at[xp]).wait()

            def convert(i, carry, xp=xp):
                split_in_two(slabs[xp * LATE + i], split, xp * 64 + EARLY + i)
                return carry

            lax.fori_loop(0, LATE, convert, 0, unroll=4)
        for xp in range(NX):
            part = split.at[pl.ds(xp * 64, EARLY)]
            pltpu.make_async_copy(part, part, early_sems.at[xp]).wait()

    for l, blocks in enumerate(refs[:2]):
        total = jnp.zeros((2 * B, 2 * HALF), jnp.float32)
        for q, off in enumerate((0, 3, 1, 2)):
            base = (l * 8 + step) * 48 + ((y + off) % NY) * 12
            left = blocks[q, 0]
            high = left.astype(jnp.bfloat16)
            low = (left - high.astype(jnp.float32)).astype(jnp.bfloat16)
            right = jnp.concatenate([split[pos[base + j]] for j in range(12)], axis=0)
            total = total + jnp.dot(
                jnp.concatenate([high, low], axis=0), right, preferred_element_type=jnp.float32
            )
        upper, lower = total[:B], total[B:]
        row_sum = upper[:, :HALF] + (upper[:, HALF:] + (lower[:, :HALF] + lower[:, HALF:]))
        out[l, 0] = row_sum
        if ahead:
            refs[-1][l * 8 + step] = row_sum
    if ahead:
        @pl.when(step == 7)
        def _():
            z, x, c = meta[0], meta[1], meta[2]
            base = (z * NX + x) * 4
            for s in range(NX):
                for j in range(8):
                    cc, l, f = j >> 2, (j >> 1) & 1, j & 1
                    row = cc * 8 + fetch[s * 2 + l, base + (c ^ cc) * 2 + f]
                    refs[5 + s][j] = refs[-1][row]


def product(meta, pos, own_blocks, partner_blocks, early, arrived, next_fetch=None):
    ahead = next_fetch is not None
    block = pl.BlockSpec((4, 1, B, 768), lambda i, *_: (0, i, 0, 0))
    anywhere = pl.BlockSpec(memory_space=pl.ANY)
    packed = jax.ShapeDtypeStruct((8, B, HALF), jnp.float32)
    return pl.pallas_call(
        functools.partial(product_kernel, int(ahead)),
        out_shape=[jax.ShapeDtypeStruct((2, 8, B, HALF), jnp.float32)] + [packed] * (NX * ahead),
        grid_spec=pltpu.PrefetchScalarGridSpec(
            num_scalar_prefetch=2 + ahead,
            grid=(8,),
            in_specs=[block] * 2 + [anywhere] * 2,
            out_specs=[pl.BlockSpec((2, 1, B, HALF), lambda i, *_: (0, i, 0, 0))]
            + [pl.BlockSpec((8, B, HALF), lambda i, *_: (0, 0, 0))] * (NX * ahead),
            scratch_shapes=[
                pltpu.VMEM((NX * LATE, B, HALF), jnp.float32),
                pltpu.VMEM((256, B, 2 * HALF), jnp.bfloat16),
                pltpu.SemaphoreType.DMA((NX,)),
                pltpu.SemaphoreType.DMA((NX,)),
            ]
            + [pltpu.VMEM((16, B, HALF), jnp.float32)] * ahead,
        ),
        name="product",
    )(meta, pos, *([next_fetch] if ahead else []), own_blocks, partner_blocks, early, arrived)


def fetch_rows(own, meta, fetch_x, ready):
    line = {0: own}
    up = down = own
    for n in range(1, 4):
        up = rows_shift(up, dz=1)
        down = rows_shift(down, dz=-1)
        line[NZ - n], line[n] = up, down
    line[4] = rows_shift(up, dz=1)
    arrived = []
    for g, offsets in enumerate(GROUPS):
        if g == 0 and ready:
            packed = ready
        else:
            packed = pack(offsets, WHOLE[g], meta, fetch_x, [line[off] for off in offsets])
        if WHOLE[g]:
            arrived.append(x_exchange(packed[0]))
            continue
        arrived.append(packed[0])
        for s in range(1, NX):
            arrived.append(rows_shift(packed[s], dx=s))
    return arrived


def turn_kernel(blocks, out):
    for t in range(6):
        out[0, :, t * 128 : (t + 1) * 128] = jnp.concatenate([blocks[0, 2 * t], blocks[0, 2 * t + 1]], axis=1)


def gather_blocks(blocks, halves):
    mine = pl.pallas_call(
        turn_kernel,
        out_shape=jax.ShapeDtypeStruct((8, B, 768), jnp.float32),
        grid=(8,),
        in_specs=[pl.BlockSpec((1, 12, B, B), lambda i: (i, 0, 0, 0))],
        out_specs=pl.BlockSpec((1, B, 768), lambda i: (i, 0, 0)),
        name="turn",
    )(blocks)
    own = [mine]
    for dy in (1, -1, 2)[: 2 if halves else 3]:
        own.append(cols_shift(mine, dy))
    if halves:
        far = []
        for n, dy in enumerate((1, -1)):
            far.append(cols_shift(own[n + 1][n * 4 : n * 4 + 4], dy))
        own.append(jnp.concatenate(far, axis=0))
    return own


def with_partner(own):
    own = jnp.stack(own)
    return own, rows_shift(own, dc=1)


def positions(slots, z, c):
    owner, f = slots // 2, slots % 2
    zp, xp, cp = owner // 8, (owner // 2) % 4, owner % 2
    l = lax.broadcasted_iota(jnp.int32, slots.shape, 0) // 8
    off = (zp - z) % NZ
    order = jnp.where(off < 4, 2 * off, jnp.where(off == 4, 7, 15 - 2 * off))
    return ((xp * NZ + order) * 8 + (cp ^ c) * 4 + l * 2 + f).reshape(-1)


def body(h_blocks, p_blocks, h_fetch, p_fetch, h_slot, p_slot, p_panel):
    r = lax.axis_index("rows").astype(jnp.int32)
    z, x, c = r // 8, (r // 2) % 4, r % 2
    meta = jnp.stack([z, x, c, lax.axis_index("cols").astype(jnp.int32)])

    pad = ((0, 0), (0, 80))
    numbers = jnp.concatenate(
        [h_fetch.reshape(1, 128), p_fetch.reshape(1, 128), jnp.pad(h_slot, pad), jnp.pad(p_slot, pad)], axis=0
    )
    other = rows_shift(numbers, dc=1)
    lists = jnp.concatenate([numbers[:2], other[:2]], axis=0)
    along = [lists]
    for s in range(1, NX):
        along.append(rows_shift(lists, dx=-s))

    left, right = p_panel[:, :HALF], p_panel[:, HALF:]
    keep, give = jnp.where(c == 0, left, right), jnp.where(c == 0, right, left)
    given = rows_shift(give, dc=1)
    own = jnp.concatenate([keep, given], axis=0).reshape(16, B, HALF)

    blocks = [gather_blocks(h_blocks, True), gather_blocks(p_blocks, False)]

    ready = None
    fetch_x = [jnp.concatenate([a[n::2] for a in along], axis=0) for n in range(2)]
    for n in range(2):
        low = 2 + 8 * n
        pos = positions(jnp.concatenate([numbers[low : low + 8, :48], other[low : low + 8, :48]], axis=0), z, c)
        arrived = fetch_rows(own, meta, fetch_x[n], ready)
        early = early_product(meta, arrived[:-1])
        own, *ready = product(meta, pos, *with_partner(blocks[n]), early, arrived[-1], fetch_x[1] if n == 0 else None)
        own = own.reshape(16, B, HALF)

    result = own.reshape(2, 512, HALF)
    back = rows_shift(result[1], dc=1)
    return jnp.where(
        c == 0,
        jnp.concatenate([result[0], back], axis=1),
        jnp.concatenate([back, result[0]], axis=1),
    )


def solution(mesh):
    in_specs = (
        P("rows", "cols", None, None),
        P("rows", "cols", None, None),
        P("rows", None, None),
        P("rows", None, None),
        P("rows", None),
        P("rows", None),
        P("rows", "cols"),
    )
    return jax.shard_map(body, mesh=mesh, in_specs=in_specs, out_specs=P("rows", "cols"), check_vma=False)
```
